1024 devices in a mesh: ctx: 16 (over z), chan: 64 (over x, y, core).
Axes of the slice: x: 4, y: 8, z: 16, core: 2. Of those that a mesh axis runs over, the one named last changes fastest.
Arguments:
- query: bfloat16 [8192, 8192], P('ctx', 'chan'), may hold values from -6 to 6
- key_in: bfloat16 [8192, 8192], P('ctx', 'chan'), may hold values from -6 to 6
- value: bfloat16 [8192, 8192], P('ctx', 'chan'), may hold values from -11 to 11
- decay: float32 [512, 16], P('chan'), may hold values from 1.2207031e-05 to 0.0333333333, as said below
- residue: float32 [512, 16], P('chan'), may hold values from -0.2 to 0.2
- skip: float32 [8192], P('chan'), may hold values from -4 to 4
- norm_gain: float32 [8192], P('chan'), may hold values from 0.1 to 1.9
Outputs:
- mixed: bfloat16 [8192, 8192], P('ctx', 'chan')
The draws below stay inside these ranges and needn't reach their ends.
Inputs may be any that keep to these rules, and one draw needn't show every extreme that they name: `decay`: rates differ from filter to filter and mode to mode.
All inputs are finite; a program needn't handle non-finite values.
Results may differ from the reference program's by a relative error of at most 0.0015.
Values sent between devices are 32-bit elements; how exact they have to be, the bound alone decides.
No kernel may reach another device: no remote copies, remote signals or barrier semaphores. Data moves between devices by JAX's collectives and lax.ppermute only.
A program may use at most 32 MiB of HBM per device.

```python
import math
import jax
import jax.numpy as jnp
from jax import lax

D = 8192
GROUP = 16
MODES = 16
GROUPS = 512
SEQ = 8192


def mode_rates(key):
    base_key = jax.random.fold_in(key, 11)
    first_key, second_key, third_key = jax.random.split(base_key, 3)
    slow_rates = jnp.exp(jax.random.uniform(first_key, (GROUPS, MODES), jnp.float32, math.log(0.1 / SEQ), math.log(2.0 / SEQ)))
    fast_rates = jnp.exp(jax.random.uniform(second_key, (GROUPS, MODES), jnp.float32, math.log(1.0 / 50.0), math.log(1.0 / 30.0)))
    share_fast = 0.5
    picked = jax.random.uniform(third_key, (GROUPS, MODES), jnp.float32) < share_fast
    return jnp.where(picked, fast_rates, slow_rates)


def draw_decay(key, part):
    return mode_rates(key)


def draw_residue(key, part):
    rates = mode_rates(key)
    own_key = jax.random.fold_in(key, 12)
    spread = jnp.clip(jax.random.normal(own_key, (GROUPS, MODES), jnp.float32), -3.0, 3.0)
    return spread * jnp.sqrt(2.0 * rates / MODES)


def draw_value(key, part):
    own_key = jax.random.fold_in(key, 21)
    base = jnp.clip(jax.random.normal(own_key, (SEQ, D), jnp.float32), -6.0, 6.0)
    ratio = math.sqrt(10.0)
    column = jnp.arange(D, dtype=jnp.float32) / (D - 1.0)
    return (base * jnp.power(ratio, column - 0.5)[None, :]).astype(jnp.bfloat16)


def level_of(key, shape, shards, smallest, top_value):
    def one(axis_at, shards_of):
        draws = jax.random.uniform(jax.random.fold_in(jax.random.fold_in(key, 6), axis_at), (shards_of,), jnp.float32, smallest / len(shards), top_value / len(shards))
        return jnp.repeat(jnp.exp(draws), shape[axis_at] // shards_of).reshape((-1,) + (1,) * (len(shape) - axis_at - 1))

    level = one(*shards[0])
    for cut in shards[1:]:
        level = level * one(*cut)
    return level


def normal_values(rng, dims, scale, reach, pieces=(), held_as=jnp.bfloat16):
    drawn = scale * jax.random.normal(rng, dims, jnp.float32)
    if pieces:
        drawn = drawn * level_of(rng, dims, pieces, -0.22, 0.18)
    return jnp.clip(drawn, -reach, reach).astype(held_as)


def setup_inputs(seed: int = 0) -> dict:
    seeds = jax.random.split(jax.random.key(seed), 8)
    query = normal_values(seeds[0], (SEQ, D), 1.0, 6.0, ((0, 16), (1, 64)))
    key_in = normal_values(seeds[1], (SEQ, D), 1.0, 6.0, ((0, 16), (1, 64)))
    value = draw_value(jax.random.fold_in(seeds[7], 71), 0)
    decay = draw_decay(jax.random.fold_in(seeds[7], 71), 0)
    residue = draw_residue(jax.random.fold_in(seeds[7], 71), 0)
    skip = normal_values(seeds[5], (D,), 1.0, 4.0, ((0, 64),), jnp.float32)
    norm_gain = jnp.clip(1.0 + 0.18 * jax.random.normal(seeds[6], (D,), jnp.float32), 0.1, 1.9)
    return {"query": query, "key_in": key_in, "value": value, "decay": decay, "residue": residue, "skip": skip, "norm_gain": norm_gain}


def reference(query, key_in, value, decay, residue, skip, norm_gain):
    gated = query.astype(jnp.float32) * key_in.astype(jnp.float32)
    rate_chan = jnp.repeat(decay, GROUP, axis=0)
    pole_chan = jnp.exp(-rate_chan)
    weight_chan = jnp.repeat(residue, GROUP, axis=0)

    def advance(state, row):
        state = pole_chan * state + row[:, None]
        return (state, lax.optimization_barrier(jnp.sum(weight_chan * state, axis=1)))
    start_state = jnp.zeros((D, MODES), jnp.float32)
    _, conv = lax.scan(advance, start_state, gated)
    out_gate = value.astype(jnp.float32) * (conv + skip[None, :] * gated)
    mean_square = lax.optimization_barrier(jnp.sum(out_gate * out_gate, axis=1, keepdims=True)) / D
    mixed = out_gate * norm_gain[None, :] * lax.rsqrt(mean_square + 1e-05)
    return mixed.astype(jnp.bfloat16)
```

```python
import jax
import jax.numpy as jnp
from jax import lax
from jax.experimental import pallas as pl
from jax.experimental.pallas import tpu as pltpu
from jax.sharding import PartitionSpec as P

D = 8192
EPS = 1e-05
CHUNK = 128
F32 = jnp.float32
BF16 = jnp.bfloat16
VMEM_BYTES = 24 << 20


def iota(shape, dim):
    return lax.broadcasted_iota(jnp.int32, shape, dim)


def split(x):
    high = x.astype(BF16)
    low = (x - high.astype(F32)).astype(BF16)
    return high, low


def dot(a, b):
    return jnp.dot(a, b, preferred_element_type=F32)


def wide_lhs(x):
    return jnp.concatenate(split(x), axis=1)


def wide_dot(lhs, x):
    pair = jnp.concatenate(split(x), axis=1)
    both = dot(lhs, jnp.concatenate([pair, pair], axis=0))
    width = x.shape[1]
    return both[:, :width] + both[:, width:]


def mode_column(table):
    groups, modes = table.shape
    rows = groups * modes
    spread = jnp.broadcast_to(table[:, None, :], (groups, modes, modes)).reshape(rows, modes)
    own = iota((rows, modes), 0) % modes == iota((rows, modes), 1)
    return jnp.sum(jnp.where(own, spread, 0.0), axis=1, keepdims=True)


def to_row(column):
    n = column.shape[0]
    diagonal = iota((n, n), 0) == iota((n, n), 1)
    return jnp.sum(jnp.where(diagonal, jnp.broadcast_to(column, (n, n)), 0.0), axis=0, keepdims=True)


def own_group(modes, width, per_group):
    rows = width // per_group * modes
    return iota((rows, width), 0) // modes == iota((rows, width), 1) // per_group


def fold(full, groups):
    rows, width = full.shape
    return jnp.sum(full.reshape(groups, rows // groups, width), axis=0)


def end_kernel(query_ref, key_ref, decay_ref, send_ref):
    tokens, width = query_ref.shape
    groups, modes = decay_ref.shape
    targets = send_ref.shape[0]
    me = lax.axis_index("ctx")
    rate = mode_column(decay_ref[...])
    mask = own_group(modes, width, width // groups)
    age = (tokens - 1 - iota((groups * modes, tokens), 1)).astype(F32)
    lhs = split(jnp.exp(-rate * age))
    gated = query_ref[...].astype(F32) * key_ref[...].astype(F32)
    high, low = split(gated)
    full = dot(lhs[0], high) + (dot(lhs[1], high) + dot(lhs[0], low))
    state = fold(jnp.where(mask, full, 0.0), groups)
    block_rate = fold(jnp.where(mask, rate * float(tokens), 0.0), groups)
    for target in range(targets):
        between = target - 1 - me
        decayed = state * jnp.exp(-block_rate * jnp.maximum(between, 0).astype(F32))
        send_ref[target] = jnp.where(between >= 0, decayed, 0.0)


def near_kernel(query_ref, key_ref, decay_ref, residue_ref, skip_ref, near_ref, far_ref):
    tokens, width = query_ref.shape
    groups, modes = decay_ref.shape
    per_group = width // groups
    rows = groups * modes
    decay, residue = decay_ref[...], residue_ref[...]
    rate = mode_column(decay)
    rate_row, residue_row = to_row(rate), to_row(mode_column(residue))
    since = (iota((tokens, rows), 0) + 1).astype(F32)
    far = wide_lhs(residue_row * jnp.exp(-rate_row * since))
    far_ref[...] = far
    lag = ((CHUNK - iota((groups, CHUNK), 1)) % CHUNK).astype(F32)
    taps = jnp.zeros((groups, CHUNK), F32)
    for m in range(modes):
        taps += residue[:, m : m + 1] * jnp.exp(-decay[:, m : m + 1] * lag)
    causal = iota((CHUNK, CHUNK), 0) >= iota((CHUNK, CHUNK), 1)
    left = []
    for g in range(groups):
        spread = jnp.broadcast_to(taps[g : g + 1], (CHUNK, CHUNK))
        turned = pltpu.roll(spread, 0, 1, stride=1, stride_axis=0)
        left.append(wide_lhs(jnp.where(causal, turned, 0.0)))
    age = (CHUNK - 1 - iota((rows, CHUNK), 1)).astype(F32)
    ends = wide_lhs(jnp.exp(-rate * age))
    step = jnp.exp(-rate * float(CHUNK))
    mask = own_group(modes, width, per_group)
    lane_group = iota((CHUNK, width), 1) // per_group
    skip = skip_ref[...]
    state = None
    for i in range(tokens // CHUNK):
        part = pl.ds(i * CHUNK, CHUNK)
        gated = query_ref[part, :].astype(F32) * key_ref[part, :].astype(F32)
        out = skip * gated
        pair = jnp.concatenate(split(gated), axis=1)
        right = jnp.concatenate([pair, pair], axis=0)
        conv = jnp.zeros((CHUNK, width), F32)
        for g in range(groups):
            both = dot(left[g], right)
            conv = jnp.where(lane_group == g, both[:, :width] + both[:, width:], conv)
        out += conv
        if state is not None:
            out += wide_dot(far[:CHUNK], state)
        near_ref[part, :] = out
        if (i + 1) * CHUNK < tokens:
            both = dot(ends, right)
            end = jnp.where(mask, both[:, :width] + both[:, width:], 0.0)
            state = end if state is None else step * state + end


def gate_kernel(got_ref, near_ref, far_ref, value_ref, out_ref, send_ref):
    tokens, width = near_ref.shape
    modes = got_ref.shape[1]
    rows = far_ref.shape[1] // 2
    groups = rows // modes
    state = got_ref[0]
    for source in range(1, got_ref.shape[0]):
        state += got_ref[source]
    mask = own_group(modes, width, width // groups)
    tiled = jnp.concatenate([state] * groups, axis=0)
    full = jnp.where(mask, tiled, 0.0)
    out = value_ref[...].astype(F32) * (near_ref[...] + wide_dot(far_ref[...], full))
    out_ref[...] = out
    squares = out * out
    sums = []
    for i in range(tokens // CHUNK):
        turned = jnp.transpose(squares[i * CHUNK : (i + 1) * CHUNK])
        sums.append(jnp.sum(turned, axis=0, keepdims=True))
    sums = jnp.concatenate(sums, axis=0)
    send_ref[...] = jnp.broadcast_to(sums[None], send_ref.shape)


def norm_kernel(got_ref, out_ref, gain_ref, mixed_ref):
    width = out_ref.shape[1]
    total = jnp.sum(got_ref[...], axis=0)
    scale = lax.rsqrt(total / D + EPS)
    for i in range(scale.shape[0]):
        part = pl.ds(i * CHUNK, CHUNK)
        column = jnp.transpose(jnp.broadcast_to(scale[i : i + 1], (width, CHUNK)))
        mixed_ref[part, :] = (out_ref[part, :] * gain_ref[...] * column).astype(BF16)


def call(kernel, outs, flops, size):
    return pl.pallas_call(
        kernel,
        out_shape=outs,
        compiler_params=pltpu.CompilerParams(vmem_limit_bytes=VMEM_BYTES),
        cost_estimate=pl.CostEstimate(flops=flops, bytes_accessed=size, transcendentals=0),
    )


def local(query, key_in, value, decay, residue, skip, norm_gain):
    tokens, width = query.shape
    groups, modes = decay.shape
    ctx, chan = lax.axis_size("ctx"), lax.axis_size("chan")
    shape = jax.ShapeDtypeStruct
    with jax.named_scope("end_state"):
        send = call(end_kernel, shape((ctx, modes, width), F32), 10**8, 10**6)(query, key_in, decay)
    with jax.named_scope("exchange_states"):
        got = lax.all_to_all(send, "ctx", 0, 0)
    with jax.named_scope("near_conv"):
        near, far = call(
            near_kernel,
            (shape((tokens, width), F32), shape((tokens, 2 * groups * modes), BF16)),
            10**9,
            4 * 10**6,
        )(query, key_in, decay, residue, skip[None, :])
    with jax.named_scope("gate"):
        out, send = call(
            gate_kernel,
            (shape((tokens, width), F32), shape((chan, tokens // CHUNK, CHUNK), F32)),
            10**8,
            10**6,
        )(got, near, far, value)
    with jax.named_scope("exchange_squares"):
        got = lax.all_to_all(send, "chan", 0, 0)
    with jax.named_scope("normalize"):
        return call(norm_kernel, shape((tokens, width), BF16), 10**6, 10**6)(
            got, out, norm_gain[None, :]
        )


def solution(mesh):
    placed = (
        P("ctx", "chan"),
        P("ctx", "chan"),
        P("ctx", "chan"),
        P("chan", None),
        P("chan", None),
        P("chan"),
        P("chan"),
    )
    return jax.shard_map(
        local, mesh=mesh, in_specs=placed, out_specs=P("ctx", "chan"), check_vma=False
    )
```

```python
import functools

import jax
import jax.numpy as jnp
from jax import lax
from jax.experimental import pallas as pl
from jax.experimental.pallas import tpu as pltpu
from jax.sharding import PartitionSpec as P

D = 8192
EPS = 1e-05
CHUNK = 128
RUN = 4
RUN_ORDER = [3, 2, 1, 0]
CHAN_FIRST = 40
F32 = jnp.float32
BF16 = jnp.bfloat16
VMEM_BYTES = 24 << 20


def iota(shape, dim):
    return lax.broadcasted_iota(jnp.int32, shape, dim)


def split(x):
    high = x.astype(BF16)
    low = (x - high.astype(F32)).astype(BF16)
    return high, low


def dot(a, b):
    return jnp.dot(a, b, preferred_element_type=F32)


def wide_lhs(x):
    return jnp.concatenate(split(x), axis=1)


def wide_dot(lhs, x):
    pair = jnp.concatenate(split(x), axis=1)
    both = dot(lhs, jnp.concatenate([pair, pair], axis=0))
    width = x.shape[1]
    return both[:, :width] + both[:, width:]


def mode_column(table):
    groups, modes = table.shape
    rows = groups * modes
    spread = jnp.broadcast_to(table[:, None, :], (groups, modes, modes)).reshape(rows, modes)
    own = iota((rows, modes), 0) % modes == iota((rows, modes), 1)
    return jnp.sum(jnp.where(own, spread, 0.0), axis=1, keepdims=True)


def to_row(column):
    n = column.shape[0]
    diagonal = iota((n, n), 0) == iota((n, n), 1)
    return jnp.sum(jnp.where(diagonal, jnp.broadcast_to(column, (n, n)), 0.0), axis=0, keepdims=True)


def own_group(modes, width, per_group):
    rows = width // per_group * modes
    return iota((rows, width), 0) // modes == iota((rows, width), 1) // per_group


def fold(full, groups):
    rows, width = full.shape
    return jnp.sum(full.reshape(groups, rows // groups, width), axis=0)


def near_part(query_ref, key_ref, decay_ref, residue_ref, skip_ref, near_ref, far_ref):
    tokens, width = query_ref.shape
    groups, modes = decay_ref.shape
    per_group = width // groups
    rows = groups * modes
    decay, residue = decay_ref[...], residue_ref[...]
    rate = mode_column(decay)
    rate_row, residue_row = to_row(rate), to_row(mode_column(residue))
    since = (iota((tokens, rows), 0) + 1).astype(F32)
    far = wide_lhs(residue_row * jnp.exp(-rate_row * since))
    far_ref[...] = far
    lag = ((CHUNK - iota((groups, CHUNK), 1)) % CHUNK).astype(F32)
    taps = jnp.zeros((groups, CHUNK), F32)
    for m in range(modes):
        taps += residue[:, m : m + 1] * jnp.exp(-decay[:, m : m + 1] * lag)
    causal = iota((CHUNK, CHUNK), 0) >= iota((CHUNK, CHUNK), 1)
    left = []
    for g in range(groups):
        spread = jnp.broadcast_to(taps[g : g + 1], (CHUNK, CHUNK))
        turned = pltpu.roll(spread, 0, 1, stride=1, stride_axis=0)
        left.append(wide_lhs(jnp.where(causal, turned, 0.0)))
    age = (CHUNK - 1 - iota((rows, CHUNK), 1)).astype(F32)
    ends = wide_lhs(jnp.exp(-rate * age))
    step = jnp.exp(-rate * float(CHUNK))
    mask = own_group(modes, width, per_group)
    lane_group = iota((CHUNK, width), 1) // per_group
    skip = skip_ref[...]
    state = None
    for i in range(tokens // CHUNK):
        part = pl.ds(i * CHUNK, CHUNK)
        gated = query_ref[part, :].astype(F32) * key_ref[part, :].astype(F32)
        out = skip * gated
        pair = jnp.concatenate(split(gated), axis=1)
        right = jnp.concatenate([pair, pair], axis=0)
        conv = jnp.zeros((CHUNK, width), F32)
        for g in range(groups):
            both = dot(left[g], right)
            conv = jnp.where(lane_group == g, both[:, :width] + both[:, width:], conv)
        out += conv
        if state is not None:
            out += wide_dot(far[:CHUNK], state)
        near_ref[part, :] = out
        if (i + 1) * CHUNK < tokens:
            both = dot(ends, right)
            end = jnp.where(mask, both[:, :width] + both[:, width:], 0.0)
            state = end if state is None else step * state + end


def first_run():
    return lax.axis_index("ctx") < RUN


def end_kernel(n, *refs):
    sources, state_ref, rate_ref = refs[:n], refs[n], refs[n + 1]
    loaded, (near_ref, far_ref), sems = refs[n + 2 : 2 * n + 2], refs[2 * n + 2 : 2 * n + 4], refs[-1]
    loads = [pltpu.make_async_copy(a, b, sems.at[i]) for i, (a, b) in enumerate(zip(sources, loaded))]
    for load in loads:
        load.start()
    decay_ref, query_ref, key_ref, residue_ref, skip_ref = loaded[:5]
    tokens, width = query_ref.shape
    groups, modes = decay_ref.shape
    loads[0].wait()
    rate = mode_column(decay_ref[...])
    mask = own_group(modes, width, width // groups)
    age = (tokens - 1 - iota((groups * modes, tokens), 1)).astype(F32)
    lhs = split(jnp.exp(-rate * age))
    rate_ref[...] = fold(jnp.where(mask, rate * float(tokens), 0.0), groups)
    loads[1].wait()
    loads[2].wait()
    gated = query_ref[...].astype(F32) * key_ref[...].astype(F32)
    high, low = split(gated)
    full = dot(lhs[0], high) + (dot(lhs[1], high) + dot(lhs[0], low))
    state_ref[...] = fold(jnp.where(mask, full, 0.0), groups)
    for load in loads[3:]:
        load.wait()

    @pl.when(first_run())
    def _():
        near_part(query_ref, key_ref, decay_ref, residue_ref, skip_ref, near_ref, far_ref)


def near_kernel(decay_ref, query_ref, key_ref, residue_ref, skip_ref, after_ref, near_ref, far_ref):
    @pl.when(jnp.logical_not(first_run()))
    def _():
        near_part(query_ref, key_ref, decay_ref, residue_ref, skip_ref, near_ref, far_ref)


def step_kernel(own_ref, rate_ref, come_ref, out_ref):
    out_ref[...] = own_ref[...] + jnp.exp(-rate_ref[...] * float(RUN)) * come_ref[...]


def hand_kernel(own_ref, rate_ref, *refs):
    earlier_refs, send_ref = refs[:-1], refs[-1]
    place = lax.axis_index("ctx") % RUN
    block_rate = rate_ref[...]
    earlier = earlier_refs[0][...]
    for ref in earlier_refs[1:]:
        earlier += ref[...]
    upto = own_ref[...] + jnp.exp(-block_rate * float(RUN)) * earlier
    for slot in range(RUN):
        between = RUN_ORDER[slot] - 1 - place
        own_run = between >= 0
        age = jnp.where(own_run, between, between + RUN).astype(F32)
        send_ref[slot] = jnp.where(own_run, upto, earlier) * jnp.exp(-block_rate * age)


def gate_kernel(got_ref, near0_ref, far0_ref, near1_ref, far1_ref, value_ref, gain_ref, out_ref, send_ref):
    tokens, width = value_ref.shape
    modes = got_ref.shape[1]
    groups = far0_ref.shape[1] // 2 // modes
    state = got_ref[0]
    for source in range(1, got_ref.shape[0]):
        state += got_ref[source]
    mask = own_group(modes, width, width // groups)
    full = jnp.where(mask, jnp.concatenate([state] * groups, axis=0), 0.0)

    def gate(near_ref, far_ref):
        out = value_ref[...].astype(F32) * (near_ref[...] + wide_dot(far_ref[...], full))
        out_ref[...] = out * gain_ref[...]
        squares = out * out
        sums = []
        for i in range(tokens // CHUNK):
            turned = jnp.transpose(squares[i * CHUNK : (i + 1) * CHUNK])
            sums.append(jnp.sum(turned, axis=0, keepdims=True))
        sums = jnp.concatenate(sums, axis=0)
        send_ref[...] = jnp.broadcast_to(sums[None], send_ref.shape)

    first = first_run()
    pl.when(first)(functools.partial(gate, near0_ref, far0_ref))
    pl.when(jnp.logical_not(first))(functools.partial(gate, near1_ref, far1_ref))


def norm_kernel(got_ref, out_ref, mixed_ref):
    width = out_ref.shape[1]
    total = jnp.sum(got_ref[...], axis=0)
    scale = lax.rsqrt(total / D + EPS)
    for i in range(scale.shape[0]):
        part = pl.ds(i * CHUNK, CHUNK)
        column = jnp.transpose(jnp.broadcast_to(scale[i : i + 1], (width, CHUNK)))
        mixed_ref[part, :] = (out_ref[part, :] * column).astype(BF16)


def call(kernel, outs, flops, size, **more):
    return pl.pallas_call(
        kernel,
        out_shape=outs,
        **more,
        compiler_params=pltpu.CompilerParams(vmem_limit_bytes=VMEM_BYTES),
        cost_estimate=pl.CostEstimate(flops=flops, bytes_accessed=size, transcendentals=0),
    )


def local(query, key_in, value, decay, residue, skip, norm_gain):
    tokens, width = query.shape
    groups, modes = decay.shape
    ctx, chan = lax.axis_size("ctx"), lax.axis_size("chan")
    shape = jax.ShapeDtypeStruct
    near_shapes = (shape((tokens, width), F32), shape((tokens, 2 * groups * modes), BF16))
    inputs = (decay, query, key_in, residue, skip[None, :], value, norm_gain[None, :])
    with jax.named_scope("end_state"):
        own, block_rate, *loaded, near0, far0 = call(
            functools.partial(end_kernel, len(inputs)),
            (
                *(shape((modes, width), F32),) * 2,
                *(shape(x.shape, x.dtype) for x in inputs),
                *near_shapes,
            ),
            10**8,
            10**6,
            in_specs=[pl.BlockSpec(memory_space=pltpu.HBM)] * len(inputs),
            scratch_shapes=[pltpu.SemaphoreType.DMA((len(inputs),))],
        )(*(pltpu.with_memory_space_constraint(x, pltpu.HBM) for x in inputs))
    *loaded, gate, gain = loaded
    with jax.named_scope("chain"):
        upto, earlier = own, []
        for run in range(1, ctx // RUN):
            links = [((run - 1) * RUN + i, run * RUN + i) for i in range(RUN)]
            come = lax.ppermute(upto, "ctx", links)
            if run == 2:
                near1, far1 = call(near_kernel, near_shapes, 10**9, 10**6)(*loaded, upto)
                come, near1, far1 = lax.optimization_barrier((come, near1, far1))
            earlier.append(come)
            if run + 1 < ctx // RUN:
                upto = call(step_kernel, shape((modes, width), F32), 10**5, 10**5)(
                    own, block_rate, come
                )
    with jax.named_scope("hand_over"):
        send = call(hand_kernel, shape((RUN, modes, width), F32), 10**6, 10**6)(
            own, block_rate, *earlier
        )
    with jax.named_scope("exchange_states"):
        runs = [[start + i for i in RUN_ORDER] for start in range(0, ctx, RUN)]
        got = lax.all_to_all(send, "ctx", 0, 0, axis_index_groups=runs)
    with jax.named_scope("gate"):
        out, send = call(
            gate_kernel,
            (shape((tokens, width), F32), shape((chan, tokens // CHUNK, CHUNK), F32)),
            10**8,
            10**6,
        )(got, near0, far0, near1, far1, gate, gain)
    with jax.named_scope("exchange_squares"):
        order = [(i + CHAN_FIRST) % chan for i in range(chan)]
        got = lax.all_to_all(send, "chan", 0, 0, axis_index_groups=[order])
    with jax.named_scope("normalize"):
        return call(norm_kernel, shape((tokens, width), BF16), 10**6, 10**6)(got, out)


def solution(mesh):
    placed = (
        P("ctx", "chan"),
        P("ctx", "chan"),
        P("ctx", "chan"),
        P("chan", None),
        P("chan", None),
        P("chan"),
        P("chan"),
    )
    return jax.shard_map(
        local, mesh=mesh, in_specs=placed, out_specs=P("ctx", "chan"), check_vma=False
    )
```

```python
import functools

import jax
import jax.numpy as jnp
from jax import lax
from jax.experimental import pallas as pl
from jax.experimental.pallas import tpu as pltpu
from jax.sharding import PartitionSpec as P

D = 8192
EPS = 1e-05
CHUNK = 128
RUN = 4
RUN_ORDER = [3, 2, 1, 0]
CHAN_FIRST = 41
F32 = jnp.float32
BF16 = jnp.bfloat16
VMEM_BYTES = 24 << 20


def iota(shape, dim):
    return lax.broadcasted_iota(jnp.int32, shape, dim)


def split(x):
    high = x.astype(BF16)
    low = (x - high.astype(F32)).astype(BF16)
    return high, low


def dot(a, b):
    return jnp.dot(a, b, preferred_element_type=F32)


def wide_lhs(x):
    return jnp.concatenate(split(x), axis=1)


def wide_dot(lhs, x):
    pair = jnp.concatenate(split(x), axis=1)
    both = dot(lhs, jnp.concatenate([pair, pair], axis=0))
    width = x.shape[1]
    return both[:, :width] + both[:, width:]


def mode_column(table):
    groups, modes = table.shape
    rows = groups * modes
    spread = jnp.broadcast_to(table[:, None, :], (groups, modes, modes)).reshape(rows, modes)
    own = iota((rows, modes), 0) % modes == iota((rows, modes), 1)
    return jnp.sum(jnp.where(own, spread, 0.0), axis=1, keepdims=True)


def to_row(column):
    n = column.shape[0]
    diagonal = iota((n, n), 0) == iota((n, n), 1)
    return jnp.sum(jnp.where(diagonal, jnp.broadcast_to(column, (n, n)), 0.0), axis=0, keepdims=True)


def own_group(modes, width, per_group):
    rows = width // per_group * modes
    return iota((rows, width), 0) // modes == iota((rows, width), 1) // per_group


def fold(full, groups):
    rows, width = full.shape
    return jnp.sum(full.reshape(groups, rows // groups, width), axis=0)


def near_part(query_ref, key_ref, decay_ref, residue_ref, skip_ref, near_ref, far_ref):
    tokens, width = query_ref.shape
    groups, modes = decay_ref.shape
    per_group = width // groups
    rows = groups * modes
    decay, residue = decay_ref[...], residue_ref[...]
    rate = mode_column(decay)
    rate_row, residue_row = to_row(rate), to_row(mode_column(residue))
    since = (iota((tokens, rows), 0) + 1).astype(F32)
    far = wide_lhs(residue_row * jnp.exp(-rate_row * since))
    far_ref[...] = far
    lag = ((CHUNK - iota((groups, CHUNK), 1)) % CHUNK).astype(F32)
    taps = jnp.zeros((groups, CHUNK), F32)
    for m in range(modes):
        taps += residue[:, m : m + 1] * jnp.exp(-decay[:, m : m + 1] * lag)
    causal = iota((CHUNK, CHUNK), 0) >= iota((CHUNK, CHUNK), 1)
    left = []
    for g in range(groups):
        spread = jnp.broadcast_to(taps[g : g + 1], (CHUNK, CHUNK))
        turned = pltpu.roll(spread, 0, 1, stride=1, stride_axis=0)
        left.append(wide_lhs(jnp.where(causal, turned, 0.0)))
    age = (CHUNK - 1 - iota((rows, CHUNK), 1)).astype(F32)
    ends = wide_lhs(jnp.exp(-rate * age))
    step = jnp.exp(-rate * float(CHUNK))
    mask = own_group(modes, width, per_group)
    lane_group = iota((CHUNK, width), 1) // per_group
    skip = skip_ref[...]
    state = None
    for i in range(tokens // CHUNK):
        part = pl.ds(i * CHUNK, CHUNK)
        gated = query_ref[part, :].astype(F32) * key_ref[part, :].astype(F32)
        out = skip * gated
        pair = jnp.concatenate(split(gated), axis=1)
        right = jnp.concatenate([pair, pair], axis=0)
        conv = jnp.zeros((CHUNK, width), F32)
        for g in range(groups):
            both = dot(left[g], right)
            conv = jnp.where(lane_group == g, both[:, :width] + both[:, width:], conv)
        out += conv
        if state is not None:
            out += wide_dot(far[:CHUNK], state)
        near_ref[part, :] = out
        if (i + 1) * CHUNK < tokens:
            both = dot(ends, right)
            end = jnp.where(mask, both[:, :width] + both[:, width:], 0.0)
            state = end if state is None else step * state + end


def first_run():
    return lax.axis_index("ctx") < RUN


def end_kernel(first, n, *refs):
    sources, state_ref, rate_ref, sems = refs[:n], refs[n], refs[n + 1], refs[-1]
    loaded = refs[n + 2 : 2 * n + 2]
    if first:
        gate_refs, (near_ref, far_ref), loaded = refs[n + 2 : n + 4], refs[n + 4 : n + 6], refs[n + 6 : -1]
        loaded = (*loaded, *gate_refs)

    @pl.when(first_run() == first)
    def _():
        loads = [
            pltpu.make_async_copy(a, b, sems.at[i]) for i, (a, b) in enumerate(zip(sources, loaded))
        ]
        for load in loads:
            load.start()
        decay_ref, query_ref, key_ref, residue_ref, skip_ref = loaded[:5]
        tokens, width = query_ref.shape
        groups, modes = decay_ref.shape
        loads[0].wait()
        rate = mode_column(decay_ref[...])
        mask = own_group(modes, width, width // groups)
        age = (tokens - 1 - iota((groups * modes, tokens), 1)).astype(F32)
        lhs = split(jnp.exp(-rate * age))
        rate_ref[...] = fold(jnp.where(mask, rate * float(tokens), 0.0), groups)
        loads[1].wait()
        loads[2].wait()
        gated = query_ref[...].astype(F32) * key_ref[...].astype(F32)
        high, low = split(gated)
        full = dot(lhs[0], high) + (dot(lhs[1], high) + dot(lhs[0], low))
        state_ref[...] = fold(jnp.where(mask, full, 0.0), groups)
        for load in loads[3:]:
            load.wait()
        if first:
            near_part(query_ref, key_ref, decay_ref, residue_ref, skip_ref, near_ref, far_ref)


def near_kernel(decay_ref, query_ref, key_ref, residue_ref, skip_ref, after_ref, near_ref, far_ref):
    @pl.when(jnp.logical_not(first_run()))
    def _():
        near_part(query_ref, key_ref, decay_ref, residue_ref, skip_ref, near_ref, far_ref)


def step_kernel(own_ref, rate_ref, come_ref, out_ref):
    out_ref[...] = own_ref[...] + jnp.exp(-rate_ref[...] * float(RUN)) * come_ref[...]


def hand_kernel(own0_ref, rate0_ref, own1_ref, rate1_ref, come_ref, rate_ref, send_ref):
    first = first_run()
    block_rate = jnp.where(first, rate0_ref[...], rate1_ref[...])
    own = jnp.where(first, own0_ref[...], own1_ref[...])
    come = come_ref[...]
    rate_ref[...] = block_rate
    modes = own.shape[0]
    upto = own + jnp.exp(-block_rate * float(RUN)) * come
    for slot in range(RUN):
        send_ref[slot, :modes] = upto
        send_ref[slot, modes:] = come


def run_kernel(got_ref, rate_ref, before_ref, total_ref):
    place = lax.axis_index("ctx") % RUN
    block_rate = rate_ref[...]
    modes = block_rate.shape[0]
    before = jnp.zeros_like(block_rate)
    total = jnp.zeros_like(block_rate)
    for slot, source in enumerate(RUN_ORDER):
        upto, come = got_ref[slot, :modes], got_ref[slot, modes:]
        between = place - 1 - source
        inside = between >= 0
        age = jnp.where(inside, between, between + RUN).astype(F32)
        before += jnp.where(inside, upto, come) * jnp.exp(-block_rate * age)
        total += upto * jnp.exp(-block_rate * float(RUN - 1 - source))
    before_ref[...] = before
    total_ref[...] = total


def gate_kernel(n, before_ref, rate_ref, *refs):
    come_refs, first_refs, other_refs = refs[:n], refs[n : n + 4], refs[n + 4 : n + 8]
    out_ref, send_ref = refs[n + 8 :]
    tokens, width = out_ref.shape
    modes = rate_ref.shape[0]
    groups = first_refs[1].shape[1] // 2 // modes
    come = come_refs[0][...]
    for ref in come_refs[1:]:
        come += ref[...]
    place = (lax.axis_index("ctx") % RUN).astype(F32)
    state = before_ref[...] + come * jnp.exp(-rate_ref[...] * place)
    mask = own_group(modes, width, width // groups)
    full = jnp.where(mask, jnp.concatenate([state] * groups, axis=0), 0.0)

    def gate(near_ref, far_ref, value_ref, gain_ref):
        out = value_ref[...].astype(F32) * (near_ref[...] + wide_dot(far_ref[...], full))
        out_ref[...] = out * gain_ref[...]
        squares = out * out
        sums = []
        for i in range(tokens // CHUNK):
            turned = jnp.transpose(squares[i * CHUNK : (i + 1) * CHUNK])
            sums.append(jnp.sum(turned, axis=0, keepdims=True))
        sums = jnp.concatenate(sums, axis=0)
        send_ref[...] = jnp.broadcast_to(sums[None], send_ref.shape)

    first = first_run()
    pl.when(first)(functools.partial(gate, *first_refs))
    pl.when(jnp.logical_not(first))(functools.partial(gate, *other_refs))


def norm_kernel(got_ref, out_ref, mixed_ref):
    width = out_ref.shape[1]
    total = jnp.sum(got_ref[...], axis=0)
    scale = lax.rsqrt(total / D + EPS)
    for i in range(scale.shape[0]):
        part = pl.ds(i * CHUNK, CHUNK)
        column = jnp.transpose(jnp.broadcast_to(scale[i : i + 1], (width, CHUNK)))
        mixed_ref[part, :] = (out_ref[part, :] * column).astype(BF16)


def call(kernel, outs, flops, size, **more):
    return pl.pallas_call(
        kernel,
        out_shape=outs,
        **more,
        compiler_params=pltpu.CompilerParams(vmem_limit_bytes=VMEM_BYTES),
        cost_estimate=pl.CostEstimate(flops=flops, bytes_accessed=size, transcendentals=0),
    )


def local(query, key_in, value, decay, residue, skip, norm_gain):
    tokens, width = query.shape
    groups, modes = decay.shape
    ctx, chan = lax.axis_size("ctx"), lax.axis_size("chan")
    shape = jax.ShapeDtypeStruct
    near_shapes = (shape((tokens, width), F32), shape((tokens, 2 * groups * modes), BF16))
    inputs = (decay, query, key_in, residue, skip[None, :], value, norm_gain[None, :])
    state_shape = shape((modes, width), F32)

    def end_state(first):
        kept = len(inputs) - 2 if first else 0
        return call(
            functools.partial(end_kernel, first, len(inputs)),
            (
                state_shape,
                state_shape,
                *(shape(x.shape, x.dtype) for x in inputs[kept:]),
                *(near_shapes if first else ()),
            ),
            10**8,
            10**6,
            in_specs=[pl.BlockSpec(memory_space=pltpu.HBM)] * len(inputs),
            scratch_shapes=[
                *(pltpu.VMEM(x.shape, x.dtype) for x in inputs[:kept]),
                pltpu.SemaphoreType.DMA((len(inputs),)),
            ],
        )(*(pltpu.with_memory_space_constraint(x, pltpu.HBM) for x in inputs))

    with jax.named_scope("end_state"):
        own0, rate0, gate0, gain0, near0, far0 = end_state(True)
        own0, rate0, inputs = lax.optimization_barrier((own0, rate0, inputs))
        come = lax.ppermute(own0, "ctx", [(i, RUN + i) for i in range(RUN)])
        own1, rate1, *loaded, gate1, gain1 = end_state(False)
    with jax.named_scope("exchange_in_run"):
        block_rate, send = call(
            hand_kernel, (state_shape, shape((RUN, 2 * modes, width), F32)), 10**5, 10**5
        )(own0, rate0, own1, rate1, come)
        runs = [[start + i for i in RUN_ORDER] for start in range(0, ctx, RUN)]
        got = lax.all_to_all(send, "ctx", 0, 0, axis_index_groups=runs)
        before, total = call(run_kernel, (state_shape,) * 2, 10**5, 10**5)(got, block_rate)
    with jax.named_scope("chain"):
        upto, come = total, []
        for run in range(2, ctx // RUN):
            if come:
                upto = call(step_kernel, state_shape, 10**5, 10**5)(total, block_rate, come[-1])
            links = [((run - 1) * RUN + i, run * RUN + i) for i in range(RUN)]
            come.append(lax.ppermute(upto, "ctx", links))
            if run == 2:
                near1, far1 = call(near_kernel, near_shapes, 10**9, 10**6)(*loaded, upto)
                come[0], near1, far1 = lax.optimization_barrier((come[0], near1, far1))
    with jax.named_scope("gate"):
        out, send = call(
            functools.partial(gate_kernel, len(come)),
            (shape((tokens, width), F32), shape((chan, tokens // CHUNK, CHUNK), F32)),
            10**8,
            10**6,
        )(before, block_rate, *come, near0, far0, gate0, gain0, near1, far1, gate1, gain1)
    with jax.named_scope("exchange_squares"):
        order = [(i + CHAN_FIRST) % chan for i in range(chan)]
        got = lax.all_to_all(send, "chan", 0, 0, axis_index_groups=[order])
    with jax.named_scope("normalize"):
        return call(norm_kernel, shape((tokens, width), BF16), 10**6, 10**6)(got, out)


def solution(mesh):
    placed = (
        P("ctx", "chan"),
        P("ctx", "chan"),
        P("ctx", "chan"),
        P("chan", None),
        P("chan", None),
        P("chan"),
        P("chan"),
    )
    return jax.shard_map(
        local, mesh=mesh, in_specs=placed, out_specs=P("ctx", "chan"), check_vma=False
    )
```

```python
import functools

import jax
import jax.numpy as jnp
from jax import lax
from jax.experimental import pallas as pl
from jax.experimental.pallas import tpu as pltpu
from jax.sharding import PartitionSpec as P

D = 8192
EPS = 1e-05
CHUNK = 128
RUN = 4
RUN_ORDER = [3, 2, 1, 0]
CHAN_FIRST = 41
F32 = jnp.float32
BF16 = jnp.bfloat16
VMEM_BYTES = 24 << 20


def iota(shape, dim):
    return lax.broadcasted_iota(jnp.int32, shape, dim)


def split(x):
    high = x.astype(BF16)
    low = (x - high.astype(F32)).astype(BF16)
    return high, low


def dot(a, b):
    return jnp.dot(a, b, preferred_element_type=F32)


def wide_lhs(x):
    return jnp.concatenate(split(x), axis=1)


def wide_dot(lhs, x):
    pair = jnp.concatenate(split(x), axis=1)
    both = dot(lhs, jnp.concatenate([pair, pair], axis=0))
    width = x.shape[1]
    return both[:, :width] + both[:, width:]


def mode_column(table):
    groups, modes = table.shape
    rows = groups * modes
    spread = jnp.broadcast_to(table[:, None, :], (groups, modes, modes)).reshape(rows, modes)
    own = iota((rows, modes), 0) % modes == iota((rows, modes), 1)
    return jnp.sum(jnp.where(own, spread, 0.0), axis=1, keepdims=True)


def to_row(column):
    n = column.shape[0]
    diagonal = iota((n, n), 0) == iota((n, n), 1)
    return jnp.sum(jnp.where(diagonal, jnp.broadcast_to(column, (n, n)), 0.0), axis=0, keepdims=True)


def own_group(modes, width, per_group):
    rows = width // per_group * modes
    return iota((rows, width), 0) // modes == iota((rows, width), 1) // per_group


def fold(full, groups):
    rows, width = full.shape
    return jnp.sum(full.reshape(groups, rows // groups, width), axis=0)


def near_part(decay_ref, query_ref, key_ref, residue_ref, skip_ref, near_ref, far_ref):
    tokens, width = query_ref.shape
    groups, modes = decay_ref.shape
    per_group = width // groups
    rows = groups * modes
    decay, residue = decay_ref[...], residue_ref[...]
    rate = mode_column(decay)
    rate_row, residue_row = to_row(rate), to_row(mode_column(residue))
    since = (iota((tokens, rows), 0) + 1).astype(F32)
    far = wide_lhs(residue_row * jnp.exp(-rate_row * since))
    far_ref[...] = far
    lag = ((CHUNK - iota((groups, CHUNK), 1)) % CHUNK).astype(F32)
    taps = jnp.zeros((groups, CHUNK), F32)
    for m in range(modes):
        taps += residue[:, m : m + 1] * jnp.exp(-decay[:, m : m + 1] * lag)
    causal = iota((CHUNK, CHUNK), 0) >= iota((CHUNK, CHUNK), 1)
    left = []
    for g in range(groups):
        spread = jnp.broadcast_to(taps[g : g + 1], (CHUNK, CHUNK))
        turned = pltpu.roll(spread, 0, 1, stride=1, stride_axis=0)
        left.append(wide_lhs(jnp.where(causal, turned, 0.0)))
    age = (CHUNK - 1 - iota((rows, CHUNK), 1)).astype(F32)
    ends = wide_lhs(jnp.exp(-rate * age))
    step = jnp.exp(-rate * float(CHUNK))
    mask = own_group(modes, width, per_group)
    lane_group = iota((CHUNK, width), 1) // per_group
    skip = skip_ref[...]
    state = None
    for i in range(tokens // CHUNK):
        part = pl.ds(i * CHUNK, CHUNK)
        gated = query_ref[part, :].astype(F32) * key_ref[part, :].astype(F32)
        out = skip * gated
        pair = jnp.concatenate(split(gated), axis=1)
        right = jnp.concatenate([pair, pair], axis=0)
        conv = jnp.zeros((CHUNK, width), F32)
        for g in range(groups):
            both = dot(left[g], right)
            conv = jnp.where(lane_group == g, both[:, :width] + both[:, width:], conv)
        out += conv
        if state is not None:
            out += wide_dot(far[:CHUNK], state)
        near_ref[part, :] = out
        if (i + 1) * CHUNK < tokens:
            both = dot(ends, right)
            end = jnp.where(mask, both[:, :width] + both[:, width:], 0.0)
            state = end if state is None else step * state + end


def first_run():
    return lax.axis_index("ctx") < RUN


def end_state(sources, state_ref, rate_ref, loaded, sems):
    loads = [pltpu.make_async_copy(a, b, sems.at[i]) for i, (a, b) in enumerate(zip(sources, loaded))]
    for load in loads:
        load.start()
    decay_ref, query_ref, key_ref = loaded[:3]
    tokens, width = query_ref.shape
    groups, modes = decay_ref.shape
    loads[0].wait()
    rate = mode_column(decay_ref[...])
    mask = own_group(modes, width, width // groups)
    age = (tokens - 1 - iota((groups * modes, tokens), 1)).astype(F32)
    lhs = split(jnp.exp(-rate * age))
    rate_ref[...] = fold(jnp.where(mask, rate * float(tokens), 0.0), groups)
    loads[1].wait()
    loads[2].wait()
    gated = query_ref[...].astype(F32) * key_ref[...].astype(F32)
    high, low = split(gated)
    full = dot(lhs[0], high) + (dot(lhs[1], high) + dot(lhs[0], low))
    state_ref[...] = fold(jnp.where(mask, full, 0.0), groups)
    for load in loads[3:]:
        load.wait()


def first_kernel(n, *refs):
    @pl.when(first_run())
    def _():
        end_state(refs[:n], refs[n], refs[n + 1], refs[n + 2 : -1], refs[-1])


def other_kernel(n, *refs):
    sources, ready, refs, sems = refs[:n], refs[n : n + 5], refs[n + 5 : -1], refs[-1]
    first = first_run()
    pl.when(first)(functools.partial(near_part, *ready, *refs[-2:]))
    others = functools.partial(end_state, sources, refs[0], refs[1], refs[2:-2], sems)
    pl.when(jnp.logical_not(first))(others)


def near_kernel(decay_ref, query_ref, key_ref, residue_ref, skip_ref, after_ref, near_ref, far_ref):
    @pl.when(jnp.logical_not(first_run()))
    def _():
        near_part(decay_ref, query_ref, key_ref, residue_ref, skip_ref, near_ref, far_ref)


def step_kernel(own_ref, rate_ref, come_ref, out_ref):
    out_ref[...] = own_ref[...] + jnp.exp(-rate_ref[...] * float(RUN)) * come_ref[...]


def hand_kernel(own0_ref, rate0_ref, own1_ref, rate1_ref, come_ref, rate_ref, send_ref):
    first = first_run()
    block_rate = jnp.where(first, rate0_ref[...], rate1_ref[...])
    own = jnp.where(first, own0_ref[...], own1_ref[...])
    come = come_ref[...]
    rate_ref[...] = block_rate
    modes = own.shape[0]
    upto = own + jnp.exp(-block_rate * float(RUN)) * come
    for slot in range(RUN):
        send_ref[slot, :modes] = upto
        send_ref[slot, modes:] = come


def run_kernel(got_ref, rate_ref, before_ref, total_ref):
    place = lax.axis_index("ctx") % RUN
    block_rate = rate_ref[...]
    modes = block_rate.shape[0]
    before = jnp.zeros_like(block_rate)
    total = jnp.zeros_like(block_rate)
    for slot, source in enumerate(RUN_ORDER):
        upto, come = got_ref[slot, :modes], got_ref[slot, modes:]
        between = place - 1 - source
        inside = between >= 0
        age = jnp.where(inside, between, between + RUN).astype(F32)
        before += jnp.where(inside, upto, come) * jnp.exp(-block_rate * age)
        total += upto * jnp.exp(-block_rate * float(RUN - 1 - source))
    before_ref[...] = before
    total_ref[...] = total


def gate_kernel(n, before_ref, rate_ref, *refs):
    come_refs, first_refs, other_refs = refs[:n], refs[n : n + 4], refs[n + 4 : n + 8]
    out_ref, send_ref = refs[n + 8 :]
    tokens, width = out_ref.shape
    modes = rate_ref.shape[0]
    groups = first_refs[1].shape[1] // 2 // modes
    come = come_refs[0][...]
    for ref in come_refs[1:]:
        come += ref[...]
    place = (lax.axis_index("ctx") % RUN).astype(F32)
    state = before_ref[...] + come * jnp.exp(-rate_ref[...] * place)
    mask = own_group(modes, width, width // groups)
    full = jnp.where(mask, jnp.concatenate([state] * groups, axis=0), 0.0)

    def gate(near_ref, far_ref, value_ref, gain_ref):
        out = value_ref[...].astype(F32) * (near_ref[...] + wide_dot(far_ref[...], full))
        out_ref[...] = out * gain_ref[...]
        squares = out * out
        sums = []
        for i in range(tokens // CHUNK):
            turned = jnp.transpose(squares[i * CHUNK : (i + 1) * CHUNK])
            sums.append(jnp.sum(turned, axis=0, keepdims=True))
        sums = jnp.concatenate(sums, axis=0)
        send_ref[...] = jnp.broadcast_to(sums[None], send_ref.shape)

    first = first_run()
    pl.when(first)(functools.partial(gate, *first_refs))
    pl.when(jnp.logical_not(first))(functools.partial(gate, *other_refs))


def norm_kernel(got_ref, out_ref, mixed_ref):
    width = out_ref.shape[1]
    total = jnp.sum(got_ref[...], axis=0)
    scale = lax.rsqrt(total / D + EPS)
    for i in range(scale.shape[0]):
        part = pl.ds(i * CHUNK, CHUNK)
        column = jnp.transpose(jnp.broadcast_to(scale[i : i + 1], (width, CHUNK)))
        mixed_ref[part, :] = (out_ref[part, :] * column).astype(BF16)


def call(kernel, outs, flops, size, **more):
    return pl.pallas_call(
        kernel,
        out_shape=outs,
        **more,
        compiler_params=pltpu.CompilerParams(vmem_limit_bytes=VMEM_BYTES),
        cost_estimate=pl.CostEstimate(flops=flops, bytes_accessed=size, transcendentals=0),
    )


def local(query, key_in, value, decay, residue, skip, norm_gain):
    tokens, width = query.shape
    groups, modes = decay.shape
    ctx, chan = lax.axis_size("ctx"), lax.axis_size("chan")
    shape = jax.ShapeDtypeStruct
    near_shapes = (shape((tokens, width), F32), shape((tokens, 2 * groups * modes), BF16))
    inputs = (decay, query, key_in, residue, skip[None, :], value, norm_gain[None, :])
    state_shape = shape((modes, width), F32)

    in_hbm = [pltpu.with_memory_space_constraint(x, pltpu.HBM) for x in inputs]

    def ends(kernel, ready, more):
        n = len(inputs)
        return call(
            functools.partial(kernel, n),
            (state_shape, state_shape, *(shape(x.shape, x.dtype) for x in inputs), *more),
            10**8,
            10**6,
            in_specs=[
                *[pl.BlockSpec(memory_space=pltpu.HBM)] * n,
                *[pl.BlockSpec(memory_space=pltpu.VMEM)] * len(ready),
            ],
            scratch_shapes=[pltpu.SemaphoreType.DMA((n,))],
        )(*in_hbm, *ready)

    with jax.named_scope("end_state"):
        own0, rate0, *loaded0, gate0, gain0 = ends(first_kernel, (), ())
        come = lax.ppermute(own0, "ctx", [(i, RUN + i) for i in range(RUN)])
        own1, rate1, *loaded, gate1, gain1, near0, far0 = ends(other_kernel, loaded0, near_shapes)
    with jax.named_scope("exchange_in_run"):
        block_rate, send = call(
            hand_kernel, (state_shape, shape((RUN, 2 * modes, width), F32)), 10**5, 10**5
        )(own0, rate0, own1, rate1, come)
        runs = [[start + i for i in RUN_ORDER] for start in range(0, ctx, RUN)]
        got = lax.all_to_all(send, "ctx", 0, 0, axis_index_groups=runs)
        before, total = call(run_kernel, (state_shape,) * 2, 10**5, 10**5)(got, block_rate)
    with jax.named_scope("chain"):
        upto, come = total, []
        for run in range(2, ctx // RUN):
            if come:
                upto = call(step_kernel, state_shape, 10**5, 10**5)(total, block_rate, come[-1])
            links = [((run - 1) * RUN + i, run * RUN + i) for i in range(RUN)]
            come.append(lax.ppermute(upto, "ctx", links))
            if run == 2:
                near1, far1 = call(near_kernel, near_shapes, 10**9, 10**6)(*loaded, upto)
                come[0], near1, far1 = lax.optimization_barrier((come[0], near1, far1))
    with jax.named_scope("gate"):
        out, send = call(
            functools.partial(gate_kernel, len(come)),
            (shape((tokens, width), F32), shape((chan, tokens // CHUNK, CHUNK), F32)),
            10**8,
            10**6,
        )(before, block_rate, *come, near0, far0, gate0, gain0, near1, far1, gate1, gain1)
    with jax.named_scope("exchange_squares"):
        order = [(i + CHAN_FIRST) % chan for i in range(chan)]
        got = lax.all_to_all(send, "chan", 0, 0, axis_index_groups=[order])
    with jax.named_scope("normalize"):
        return call(norm_kernel, shape((tokens, width), BF16), 10**6, 10**6)(got, out)


def solution(mesh):
    placed = (
        P("ctx", "chan"),
        P("ctx", "chan"),
        P("ctx", "chan"),
        P("chan", None),
        P("chan", None),
        P("chan"),
        P("chan"),
    )
    return jax.shard_map(
        local, mesh=mesh, in_specs=placed, out_specs=P("ctx", "chan"), check_vma=False
    )
```

```python
import functools

import jax
import jax.numpy as jnp
from jax import lax
from jax.experimental import pallas as pl
from jax.experimental.pallas import tpu as pltpu
from jax.sharding import PartitionSpec as P

D = 8192
EPS = 1e-05
CHUNK = 128
RUN = 4
RUN_ORDER = [3, 2, 1, 0]
CHAN_FIRST = 41
F32 = jnp.float32
BF16 = jnp.bfloat16
VMEM_BYTES = 24 << 20


def iota(shape, dim):
    return lax.broadcasted_iota(jnp.int32, shape, dim)


def split(x):
    high = x.astype(BF16)
    low = (x - high.astype(F32)).astype(BF16)
    return high, low


def dot(a, b):
    return jnp.dot(a, b, preferred_element_type=F32)


def wide_lhs(x):
    return jnp.concatenate(split(x), axis=1)


def wide_dot(lhs, x):
    pair = jnp.concatenate(split(x), axis=1)
    both = dot(lhs, jnp.concatenate([pair, pair], axis=0))
    width = x.shape[1]
    return both[:, :width] + both[:, width:]


def mode_column(table):
    groups, modes = table.shape
    rows = groups * modes
    spread = jnp.broadcast_to(table[:, None, :], (groups, modes, modes)).reshape(rows, modes)
    own = iota((rows, modes), 0) % modes == iota((rows, modes), 1)
    return jnp.sum(jnp.where(own, spread, 0.0), axis=1, keepdims=True)


def to_row(column):
    n = column.shape[0]
    diagonal = iota((n, n), 0) == iota((n, n), 1)
    return jnp.sum(jnp.where(diagonal, jnp.broadcast_to(column, (n, n)), 0.0), axis=0, keepdims=True)


def own_group(modes, width, per_group):
    rows = width // per_group * modes
    return iota((rows, width), 0) // modes == iota((rows, width), 1) // per_group


def fold(full, groups):
    rows, width = full.shape
    return jnp.sum(full.reshape(groups, rows // groups, width), axis=0)


def near_part(decay_ref, query_ref, key_ref, residue_ref, skip_ref, near_ref, far_ref):
    tokens, width = query_ref.shape
    groups, modes = decay_ref.shape
    per_group = width // groups
    rows = groups * modes
    decay, residue = decay_ref[...], residue_ref[...]
    rate = mode_column(decay)
    rate_row, residue_row = to_row(rate), to_row(mode_column(residue))
    since = (iota((tokens, rows), 0) + 1).astype(F32)
    far = wide_lhs(residue_row * jnp.exp(-rate_row * since))
    far_ref[...] = far
    lag = ((CHUNK - iota((groups, CHUNK), 1)) % CHUNK).astype(F32)
    taps = jnp.zeros((groups, CHUNK), F32)
    for m in range(modes):
        taps += residue[:, m : m + 1] * jnp.exp(-decay[:, m : m + 1] * lag)
    causal = iota((CHUNK, CHUNK), 0) >= iota((CHUNK, CHUNK), 1)
    left = []
    for g in range(groups):
        spread = jnp.broadcast_to(taps[g : g + 1], (CHUNK, CHUNK))
        turned = pltpu.roll(spread, 0, 1, stride=1, stride_axis=0)
        left.append(wide_lhs(jnp.where(causal, turned, 0.0)))
    age = (CHUNK - 1 - iota((rows, CHUNK), 1)).astype(F32)
    ends = wide_lhs(jnp.exp(-rate * age))
    step = jnp.exp(-rate * float(CHUNK))
    mask = own_group(modes, width, per_group)
    lane_group = iota((CHUNK, width), 1) // per_group
    skip = skip_ref[...]
    state = None
    for i in range(tokens // CHUNK):
        part = pl.ds(i * CHUNK, CHUNK)
        gated = query_ref[part, :].astype(F32) * key_ref[part, :].astype(F32)
        out = skip * gated
        pair = jnp.concatenate(split(gated), axis=1)
        right = jnp.concatenate([pair, pair], axis=0)
        conv = jnp.zeros((CHUNK, width), F32)
        for g in range(groups):
            both = dot(left[g], right)
            conv = jnp.where(lane_group == g, both[:, :width] + both[:, width:], conv)
        out += conv
        if state is not None:
            out += wide_dot(far[:CHUNK], state)
        near_ref[part, :] = out
        if (i + 1) * CHUNK < tokens:
            both = dot(ends, right)
            end = jnp.where(mask, both[:, :width] + both[:, width:], 0.0)
            state = end if state is None else step * state + end


def first_run():
    return lax.axis_index("ctx") < RUN


def end_state(sources, state_ref, rate_ref, loaded, sems):
    loads = [pltpu.make_async_copy(a, b, sems.at[i]) for i, (a, b) in enumerate(zip(sources, loaded))]
    for load in loads:
        load.start()
    decay_ref, query_ref, key_ref = loaded[:3]
    tokens, width = query_ref.shape
    groups, modes = decay_ref.shape
    loads[0].wait()
    rate = mode_column(decay_ref[...])
    mask = own_group(modes, width, width // groups)
    age = (tokens - 1 - iota((groups * modes, tokens), 1)).astype(F32)
    lhs = split(jnp.exp(-rate * age))
    rate_ref[...] = fold(jnp.where(mask, rate * float(tokens), 0.0), groups)
    loads[1].wait()
    loads[2].wait()
    gated = query_ref[...].astype(F32) * key_ref[...].astype(F32)
    high, low = split(gated)
    full = dot(lhs[0], high) + (dot(lhs[1], high) + dot(lhs[0], low))
    state_ref[...] = fold(jnp.where(mask, full, 0.0), groups)
    for load in loads[3:]:
        load.wait()


def first_kernel(n, *refs):
    @pl.when(first_run())
    def _():
        end_state(refs[:n], refs[n], refs[n + 1], refs[n + 2 : -1], refs[-1])


def other_kernel(n, *refs):
    sources, ready, refs, sems = refs[:n], refs[n : n + 5], refs[n + 5 : -1], refs[-1]
    first = first_run()
    pl.when(first)(functools.partial(near_part, *ready, *refs[-2:]))
    others = functools.partial(end_state, sources, refs[0], refs[1], refs[2:-2], sems)
    pl.when(jnp.logical_not(first))(others)


def near_kernel(decay_ref, query_ref, key_ref, residue_ref, skip_ref, after_ref, near_ref, far_ref):
    @pl.when(jnp.logical_not(first_run()))
    def _():
        near_part(decay_ref, query_ref, key_ref, residue_ref, skip_ref, near_ref, far_ref)


def step_kernel(own_ref, rate_ref, come_ref, out_ref):
    out_ref[...] = own_ref[...] + jnp.exp(-rate_ref[...] * float(RUN)) * come_ref[...]


def hand_kernel(
    own0_ref, rate0_ref, own1_ref, rate1_ref, come_ref, oldest_ref, rate_ref, send_ref
):
    first = first_run()
    block_rate = jnp.where(first, rate0_ref[...], rate1_ref[...])
    own = jnp.where(first, own0_ref[...], own1_ref[...])
    come = come_ref[...] + jnp.exp(-block_rate) * oldest_ref[...]
    rate_ref[...] = block_rate
    modes = own.shape[0]
    upto = own + jnp.exp(-block_rate * float(RUN - 1)) * come
    for slot in range(RUN):
        send_ref[slot, :modes] = upto
        send_ref[slot, modes:] = come


def run_kernel(got_ref, rate_ref, before_ref, total_ref):
    place = lax.axis_index("ctx") % RUN
    block_rate = rate_ref[...]
    modes = block_rate.shape[0]
    before = jnp.zeros_like(block_rate)
    total = jnp.zeros_like(block_rate)
    for slot, source in enumerate(RUN_ORDER):
        upto, come = got_ref[slot, :modes], got_ref[slot, modes:]
        between = place - 1 - source
        inside = between >= 0
        age = jnp.maximum(jnp.where(inside, between, between + RUN - 1), 0).astype(F32)
        before += jnp.where(inside, upto, come) * jnp.exp(-block_rate * age)
        total += upto * jnp.exp(-block_rate * float(RUN - 1 - source))
    before_ref[...] = before
    total_ref[...] = total


def gate_kernel(n, before_ref, rate_ref, *refs):
    come_refs, first_refs, other_refs = refs[:n], refs[n : n + 4], refs[n + 4 : n + 8]
    out_ref, send_ref = refs[n + 8 :]
    tokens, width = out_ref.shape
    modes = rate_ref.shape[0]
    groups = first_refs[1].shape[1] // 2 // modes
    come = come_refs[0][...]
    for ref in come_refs[1:]:
        come += ref[...]
    place = (lax.axis_index("ctx") % RUN).astype(F32)
    state = before_ref[...] + come * jnp.exp(-rate_ref[...] * place)
    mask = own_group(modes, width, width // groups)
    full = jnp.where(mask, jnp.concatenate([state] * groups, axis=0), 0.0)

    def gate(near_ref, far_ref, value_ref, gain_ref):
        out = value_ref[...].astype(F32) * (near_ref[...] + wide_dot(far_ref[...], full))
        out_ref[...] = out * gain_ref[...]
        squares = out * out
        sums = []
        for i in range(tokens // CHUNK):
            turned = jnp.transpose(squares[i * CHUNK : (i + 1) * CHUNK])
            sums.append(jnp.sum(turned, axis=0, keepdims=True))
        sums = jnp.concatenate(sums, axis=0)
        send_ref[...] = jnp.broadcast_to(sums[None], send_ref.shape)

    first = first_run()
    pl.when(first)(functools.partial(gate, *first_refs))
    pl.when(jnp.logical_not(first))(functools.partial(gate, *other_refs))


def norm_kernel(got_ref, out_ref, mixed_ref):
    parts = got_ref[...]
    while parts.shape[0] > 1:
        half = parts.shape[0] // 2
        parts = parts[:half] + parts[half:]
    scale = lax.rsqrt(parts[0] / D + EPS)
    columns = jnp.transpose(jnp.concatenate([scale, scale], axis=0))
    for i in range(scale.shape[0]):
        part = pl.ds(i * CHUNK, CHUNK)
        mixed_ref[part, :] = (out_ref[part, :] * columns[:, i : i + 1]).astype(BF16)


def call(kernel, outs, flops, size, **more):
    return pl.pallas_call(
        kernel,
        out_shape=outs,
        **more,
        compiler_params=pltpu.CompilerParams(vmem_limit_bytes=VMEM_BYTES),
        cost_estimate=pl.CostEstimate(flops=flops, bytes_accessed=size, transcendentals=0),
    )


def local(query, key_in, value, decay, residue, skip, norm_gain):
    tokens, width = query.shape
    groups, modes = decay.shape
    ctx, chan = lax.axis_size("ctx"), lax.axis_size("chan")
    shape = jax.ShapeDtypeStruct
    near_shapes = (shape((tokens, width), F32), shape((tokens, 2 * groups * modes), BF16))
    inputs = (decay, query, key_in, residue, skip[None, :], value, norm_gain[None, :])
    state_shape = shape((modes, width), F32)

    in_hbm = [pltpu.with_memory_space_constraint(x, pltpu.HBM) for x in inputs]

    def ends(kernel, ready, more):
        n = len(inputs)
        return call(
            functools.partial(kernel, n),
            (state_shape, state_shape, *(shape(x.shape, x.dtype) for x in inputs), *more),
            10**8,
            10**6,
            in_specs=[
                *[pl.BlockSpec(memory_space=pltpu.HBM)] * n,
                *[pl.BlockSpec(memory_space=pltpu.VMEM)] * len(ready),
            ],
            scratch_shapes=[pltpu.SemaphoreType.DMA((n,))],
        )(*in_hbm, *ready)

    with jax.named_scope("end_state"):
        own0, rate0, *loaded0, gate0, gain0 = ends(first_kernel, (), ())
        oldest = lax.ppermute(own0, "ctx", [(0, RUN)])
        come = lax.ppermute(own0, "ctx", [(i, RUN - 1 + i) for i in range(1, RUN)])
        own1, rate1, *loaded, gate1, gain1, near0, far0 = ends(other_kernel, loaded0, near_shapes)
    with jax.named_scope("exchange_in_run"):
        block_rate, send = call(
            hand_kernel, (state_shape, shape((RUN, 2 * modes, width), F32)), 10**5, 10**5
        )(own0, rate0, own1, rate1, come, oldest)
        runs = [[start + i for i in RUN_ORDER] for start in range(0, ctx, RUN)]
        got = lax.all_to_all(send, "ctx", 0, 0, axis_index_groups=runs)
        before, total = call(run_kernel, (state_shape,) * 2, 10**5, 10**5)(got, block_rate)
    with jax.named_scope("chain"):
        upto, come = total, []
        for run in range(2, ctx // RUN):
            if come:
                upto = call(step_kernel, state_shape, 10**5, 10**5)(total, block_rate, come[-1])
            links = [((run - 1) * RUN + i, run * RUN + i) for i in range(RUN)]
            come.append(lax.ppermute(upto, "ctx", links))
            if run == 2:
                near1, far1 = call(near_kernel, near_shapes, 10**9, 10**6)(*loaded, upto)
                come[0], near1, far1 = lax.optimization_barrier((come[0], near1, far1))
    with jax.named_scope("gate"):
        out, send = call(
            functools.partial(gate_kernel, len(come)),
            (shape((tokens, width), F32), shape((chan, tokens // CHUNK, CHUNK), F32)),
            10**8,
            10**6,
        )(before, block_rate, *come, near0, far0, gate0, gain0, near1, far1, gate1, gain1)
    with jax.named_scope("exchange_squares"):
        order = [(i + CHAN_FIRST) % chan for i in range(chan)]
        got = lax.all_to_all(send, "chan", 0, 0, axis_index_groups=[order])
    with jax.named_scope("normalize"):
        return call(norm_kernel, shape((tokens, width), BF16), 10**6, 10**6)(got, out)


def solution(mesh):
    placed = (
        P("ctx", "chan"),
        P("ctx", "chan"),
        P("ctx", "chan"),
        P("chan", None),
        P("chan", None),
        P("chan"),
        P("chan"),
    )
    return jax.shard_map(
        local, mesh=mesh, in_specs=placed, out_specs=P("ctx", "chan"), check_vma=False
    )
```

```python
import functools

import jax
import jax.numpy as jnp
from jax import lax
from jax.experimental import pallas as pl
from jax.experimental.pallas import tpu as pltpu
from jax.sharding import PartitionSpec as P

D = 8192
EPS = 1e-05
CHUNK = 128
RUN = 4
RUN_ORDER = [3, 2, 1, 0]
CHAN_FIRST = 41
F32 = jnp.float32
BF16 = jnp.bfloat16
VMEM_BYTES = 24 << 20


def iota(shape, dim):
    return lax.broadcasted_iota(jnp.int32, shape, dim)


def split(x):
    high = x.astype(BF16)
    low = (x - high.astype(F32)).astype(BF16)
    return high, low


def dot(a, b):
    return jnp.dot(a, b, preferred_element_type=F32)


def wide_lhs(x):
    return jnp.concatenate(split(x), axis=1)


def wide_dot(lhs, x):
    pair = jnp.concatenate(split(x), axis=1)
    both = dot(lhs, jnp.concatenate([pair, pair], axis=0))
    width = x.shape[1]
    return both[:, :width] + both[:, width:]


def mode_column(table):
    groups, modes = table.shape
    rows = groups * modes
    spread = jnp.broadcast_to(table[:, None, :], (groups, modes, modes)).reshape(rows, modes)
    own = iota((rows, modes), 0) % modes == iota((rows, modes), 1)
    return jnp.sum(jnp.where(own, spread, 0.0), axis=1, keepdims=True)


def to_row(column):
    n = column.shape[0]
    diagonal = iota((n, n), 0) == iota((n, n), 1)
    return jnp.sum(jnp.where(diagonal, jnp.broadcast_to(column, (n, n)), 0.0), axis=0, keepdims=True)


def own_group(modes, width, per_group):
    rows = width // per_group * modes
    return iota((rows, width), 0) // modes == iota((rows, width), 1) // per_group


def fold(full, groups):
    rows, width = full.shape
    return jnp.sum(full.reshape(groups, rows // groups, width), axis=0)


def near_part(decay_ref, query_ref, key_ref, residue_ref, skip_ref, near_ref, far_ref):
    tokens, width = query_ref.shape
    groups, modes = decay_ref.shape
    per_group = width // groups
    rows = groups * modes
    decay, residue = decay_ref[...], residue_ref[...]
    rate = mode_column(decay)
    rate_row, residue_row = to_row(rate), to_row(mode_column(residue))
    since = (iota((tokens, rows), 0) + 1).astype(F32)
    far = wide_lhs(residue_row * jnp.exp(-rate_row * since))
    far_ref[...] = far
    lag = ((CHUNK - iota((groups, CHUNK), 1)) % CHUNK).astype(F32)
    taps = jnp.zeros((groups, CHUNK), F32)
    for m in range(modes):
        taps += residue[:, m : m + 1] * jnp.exp(-decay[:, m : m + 1] * lag)
    causal = iota((CHUNK, CHUNK), 0) >= iota((CHUNK, CHUNK), 1)
    left = []
    for g in range(groups):
        spread = jnp.broadcast_to(taps[g : g + 1], (CHUNK, CHUNK))
        turned = pltpu.roll(spread, 0, 1, stride=1, stride_axis=0)
        left.append(wide_lhs(jnp.where(causal, turned, 0.0)))
    age = (CHUNK - 1 - iota((rows, CHUNK), 1)).astype(F32)
    ends = wide_lhs(jnp.exp(-rate * age))
    step = jnp.exp(-rate * float(CHUNK))
    mask = own_group(modes, width, per_group)
    lane_group = iota((CHUNK, width), 1) // per_group
    skip = skip_ref[...]
    state = None
    for i in range(tokens // CHUNK):
        part = pl.ds(i * CHUNK, CHUNK)
        gated = query_ref[part, :].astype(F32) * key_ref[part, :].astype(F32)
        out = skip * gated
        pair = jnp.concatenate(split(gated), axis=1)
        right = jnp.concatenate([pair, pair], axis=0)
        conv = jnp.zeros((CHUNK, width), F32)
        for g in range(groups):
            both = dot(left[g], right)
            conv = jnp.where(lane_group == g, both[:, :width] + both[:, width:], conv)
        out += conv
        if state is not None:
            out += wide_dot(far[:CHUNK], state)
        near_ref[part, :] = out
        if (i + 1) * CHUNK < tokens:
            both = dot(ends, right)
            end = jnp.where(mask, both[:, :width] + both[:, width:], 0.0)
            state = end if state is None else step * state + end


def first_run():
    return lax.axis_index("ctx") < RUN


def end_state(sources, state_ref, rate_ref, loaded, sems):
    loads = [pltpu.make_async_copy(a, b, sems.at[i]) for i, (a, b) in enumerate(zip(sources, loaded))]
    for load in loads:
        load.start()
    decay_ref, query_ref, key_ref = loaded[:3]
    tokens, width = query_ref.shape
    groups, modes = decay_ref.shape
    loads[0].wait()
    rate = mode_column(decay_ref[...])
    mask = own_group(modes, width, width // groups)
    age = (tokens - 1 - iota((groups * modes, tokens), 1)).astype(F32)
    lhs = split(jnp.exp(-rate * age))
    rate_ref[...] = fold(jnp.where(mask, rate * float(tokens), 0.0), groups)
    loads[1].wait()
    loads[2].wait()
    gated = query_ref[...].astype(F32) * key_ref[...].astype(F32)
    high, low = split(gated)
    full = dot(lhs[0], high) + (dot(lhs[1], high) + dot(lhs[0], low))
    state_ref[...] = fold(jnp.where(mask, full, 0.0), groups)
    for load in loads[3:]:
        load.wait()


def first_kernel(n, *refs):
    @pl.when(first_run())
    def _():
        end_state(refs[:n], refs[n], refs[n + 1], refs[n + 2 : -1], refs[-1])


def other_kernel(n, *refs):
    sources, ready, refs, sems = refs[:n], refs[n : n + 5], refs[n + 5 : -1], refs[-1]
    first = first_run()
    pl.when(first)(functools.partial(near_part, *ready, *refs[-2:]))
    others = functools.partial(end_state, sources, refs[0], refs[1], refs[2:-2], sems)
    pl.when(jnp.logical_not(first))(others)


def near_kernel(decay_ref, query_ref, key_ref, residue_ref, skip_ref, after_ref, near_ref, far_ref):
    @pl.when(jnp.logical_not(first_run()))
    def _():
        near_part(decay_ref, query_ref, key_ref, residue_ref, skip_ref, near_ref, far_ref)


def step_kernel(own_ref, rate_ref, come_ref, out_ref):
    out_ref[...] = own_ref[...] + jnp.exp(-rate_ref[...] * float(RUN)) * come_ref[...]


def hand_kernel(own0_ref, rate0_ref, own1_ref, rate1_ref, come_ref, rate_ref, send_ref):
    first = first_run()
    block_rate = jnp.where(first, rate0_ref[...], rate1_ref[...])
    own = jnp.where(first, own0_ref[...], own1_ref[...])
    come = come_ref[...]
    rate_ref[...] = block_rate
    modes = own.shape[0]
    upto = own + jnp.exp(-block_rate * float(RUN)) * come
    for slot in range(RUN):
        send_ref[slot, :modes] = upto
        send_ref[slot, modes:] = come


def run_kernel(got_ref, rate_ref, before_ref, total_ref):
    place = lax.axis_index("ctx") % RUN
    block_rate = rate_ref[...]
    modes = block_rate.shape[0]
    before = jnp.zeros_like(block_rate)
    total = jnp.zeros_like(block_rate)
    for slot, source in enumerate(RUN_ORDER):
        upto, come = got_ref[slot, :modes], got_ref[slot, modes:]
        between = place - 1 - source
        inside = between >= 0
        age = jnp.where(inside, between, between + RUN).astype(F32)
        before += jnp.where(inside, upto, come) * jnp.exp(-block_rate * age)
        total += upto * jnp.exp(-block_rate * float(RUN - 1 - source))
    before_ref[...] = before
    total_ref[...] = total


def gate_kernel(n, before_ref, rate_ref, *refs):
    come_refs, first_refs, other_refs = refs[:n], refs[n : n + 4], refs[n + 4 : n + 8]
    out_ref, send_ref = refs[n + 8 :]
    tokens, width = out_ref.shape
    modes = rate_ref.shape[0]
    groups = first_refs[1].shape[1] // 2 // modes
    come = come_refs[0][...]
    for ref in come_refs[1:]:
        come += ref[...]
    place = (lax.axis_index("ctx") % RUN).astype(F32)
    state = before_ref[...] + come * jnp.exp(-rate_ref[...] * place)
    mask = own_group(modes, width, width // groups)
    full = jnp.where(mask, jnp.concatenate([state] * groups, axis=0), 0.0)

    def gate(near_ref, far_ref, value_ref, gain_ref):
        out = value_ref[...].astype(F32) * (near_ref[...] + wide_dot(far_ref[...], full))
        out_ref[...] = out * gain_ref[...]
        squares = out * out
        sums = []
        for i in range(tokens // CHUNK):
            turned = jnp.transpose(squares[i * CHUNK : (i + 1) * CHUNK])
            sums.append(jnp.sum(turned, axis=0, keepdims=True))
        sums = jnp.concatenate(sums, axis=0)
        send_ref[...] = jnp.broadcast_to(sums[None], send_ref.shape)

    first = first_run()
    pl.when(first)(functools.partial(gate, *first_refs))
    pl.when(jnp.logical_not(first))(functools.partial(gate, *other_refs))


def norm_kernel(got_ref, out_ref, mixed_ref):
    parts = got_ref[...]
    while parts.shape[0] > 1:
        half = parts.shape[0] // 2
        parts = parts[:half] + parts[half:]
    scale = lax.rsqrt(parts[0] / D + EPS)
    columns = jnp.transpose(jnp.concatenate([scale, scale], axis=0))
    for i in range(scale.shape[0]):
        part = pl.ds(i * CHUNK, CHUNK)
        mixed_ref[part, :] = (out_ref[part, :] * columns[:, i : i + 1]).astype(BF16)


def call(kernel, outs, flops, size, **more):
    return pl.pallas_call(
        kernel,
        out_shape=outs,
        **more,
        compiler_params=pltpu.CompilerParams(vmem_limit_bytes=VMEM_BYTES),
        cost_estimate=pl.CostEstimate(flops=flops, bytes_accessed=size, transcendentals=0),
    )


def local(query, key_in, value, decay, residue, skip, norm_gain):
    tokens, width = query.shape
    groups, modes = decay.shape
    ctx, chan = lax.axis_size("ctx"), lax.axis_size("chan")
    shape = jax.ShapeDtypeStruct
    near_shapes = (shape((tokens, width), F32), shape((tokens, 2 * groups * modes), BF16))
    inputs = (decay, query, key_in, residue, skip[None, :], value, norm_gain[None, :])
    state_shape = shape((modes, width), F32)

    in_hbm = [pltpu.with_memory_space_constraint(x, pltpu.HBM) for x in inputs]

    def ends(kernel, ready, more):
        n = len(inputs)
        return call(
            functools.partial(kernel, n),
            (state_shape, state_shape, *(shape(x.shape, x.dtype) for x in inputs), *more),
            10**8,
            10**6,
            in_specs=[
                *[pl.BlockSpec(memory_space=pltpu.HBM)] * n,
                *[pl.BlockSpec(memory_space=pltpu.VMEM)] * len(ready),
            ],
            scratch_shapes=[pltpu.SemaphoreType.DMA((n,))],
        )(*in_hbm, *ready)

    with jax.named_scope("end_state"):
        own0, rate0, *loaded0, gate0, gain0 = ends(first_kernel, (), ())
        come = lax.ppermute(own0, "ctx", [(i, RUN + i) for i in range(RUN)])
        own1, rate1, *loaded, gate1, gain1, near0, far0 = ends(other_kernel, loaded0, near_shapes)
    with jax.named_scope("exchange_in_run"):
        block_rate, send = call(
            hand_kernel, (state_shape, shape((RUN, 2 * modes, width), F32)), 10**5, 10**5
        )(own0, rate0, own1, rate1, come)
        runs = [[start + i for i in RUN_ORDER] for start in range(0, ctx, RUN)]
        got = lax.all_to_all(send, "ctx", 0, 0, axis_index_groups=runs)
        before, total = call(run_kernel, (state_shape,) * 2, 10**5, 10**5)(got, block_rate)
    with jax.named_scope("chain"):
        upto, come = total, []
        for run in range(2, ctx // RUN):
            if come:
                upto = call(step_kernel, state_shape, 10**5, 10**5)(total, block_rate, come[-1])
            links = [((run - 1) * RUN + i, run * RUN + i) for i in range(RUN)]
            come.append(lax.ppermute(upto, "ctx", links))
            if run == 2:
                near1, far1 = call(near_kernel, near_shapes, 10**9, 10**6)(*loaded, upto)
                come[0], near1, far1 = lax.optimization_barrier((come[0], near1, far1))
    with jax.named_scope("gate"):
        out, send = call(
            functools.partial(gate_kernel, len(come)),
            (shape((tokens, width), F32), shape((chan, tokens // CHUNK, CHUNK), F32)),
            10**8,
            10**6,
        )(before, block_rate, *come, near0, far0, gate0, gain0, near1, far1, gate1, gain1)
    with jax.named_scope("exchange_squares"):
        order = [(i + CHAN_FIRST) % chan for i in range(chan)]
        got = lax.all_to_all(send, "chan", 0, 0, axis_index_groups=[order])
    with jax.named_scope("normalize"):
        return call(norm_kernel, shape((tokens, width), BF16), 10**6, 10**6)(got, out)


def solution(mesh):
    placed = (
        P("ctx", "chan"),
        P("ctx", "chan"),
        P("ctx", "chan"),
        P("chan", None),
        P("chan", None),
        P("chan"),
        P("chan"),
    )
    return jax.shard_map(
        local, mesh=mesh, in_specs=placed, out_specs=P("ctx", "chan"), check_vma=False
    )
```
